32 devices in a mesh: leaf: 8 (over z, y), sub: 4 (over x, core).
Axes of the slice: x: 2, y: 2, z: 4, core: 2. Of those that a mesh axis runs over, the one named last changes fastest.
Arguments:
- sources: bfloat16 [65536, 64], P(('leaf', 'sub')), may hold values from -6 to 6
- leaf_basis: bfloat16 [256, 256, 64], P(('leaf', 'sub')), may hold values from -0.375 to 0.375
- transfer: float32 [2, 64, 64], replicated, may hold values from -0.625 to 0.625
- coupling: float32 [3, 64, 64], replicated, may hold values from -0.5 to 0.5
- near_blocks: bfloat16 [256, 4, 256, 256], P(('leaf', 'sub')), may hold values from -0.1875 to 0.1875
- near_pattern: int32 [256, 4], P(('leaf', 'sub')), may hold values from 0 to 255, as said below
- far_pattern: int32 [508, 3], replicated, may hold values 0 or 1
Outputs:
- product: bfloat16 [65536, 64], P(('leaf', 'sub'))
The draws below stay inside these ranges and needn't reach their ends.
Inputs may be any that keep to these rules, and one draw needn't show every extreme that they name: near_pattern[i, 0] = i; every entry j has j // 8 - i // 8 equal to 0, 1, -1, 4 or -4.
All inputs are finite; a program needn't handle non-finite values.
Results may differ from the reference program's by a relative error of at most 0.001.
Values may be sent and summed in bfloat16 or wider, within the bound.
A program may use at most 64 MiB of HBM per device.

```python
import jax
import jax.numpy as jnp
from jax import lax

LEAF_PTS = 256
RANK = 64
RHS = 64
NEAR = 4
LEAF_DEV = 8
SUB_SPAN = 4
LEAVES = 256
POINTS = 65536
FAR_ROWS = 508


def draw_near_pattern(key, part):
    leaf_ids = jnp.arange(LEAVES, dtype=jnp.int32)
    device_ids = leaf_ids // LEAF_DEV
    device_total = LEAVES // LEAF_DEV
    key_side, key_leaf = jax.random.split(jax.random.fold_in(key, 17))
    direction = jax.random.randint(key_side, (LEAVES, NEAR), 0, 5)
    steps_table = jnp.array([0, -1, 1, -SUB_SPAN, SUB_SPAN], jnp.int32)
    target = device_ids[:, None] + steps_table[direction]
    target = jnp.where((target < 0) | (target >= device_total), device_ids[:, None], target)
    within = jax.random.randint(key_leaf, (LEAVES, NEAR), 0, LEAF_DEV)
    chosen = (target * LEAF_DEV + within).astype(jnp.int32)
    return chosen.at[:, 0].set(leaf_ids)


def touch_ends(values, stream_key, smallest, top_value):
    shape = values.shape
    place = [jax.random.randint(jax.random.fold_in(stream_key, axis), (), 0, shape[axis]) for axis in range(len(shape))]
    values = values.at[tuple(place)].set(smallest)
    longest = shape.index(max(shape))
    place[longest] = (place[longest] + 1) % shape[longest]
    return values.at[tuple(place)].set(top_value)


def levels(own_key, dims, cuts, smallest, largest):
    factor_of, own = 1.0, jax.random.fold_in(own_key, 6)
    for position, blocks in cuts:
        heights = jnp.exp(jax.random.uniform(jax.random.fold_in(own, position), (blocks,), jnp.float32, smallest / len(cuts), largest / len(cuts)))
        factor_of = factor_of * jnp.repeat(heights, dims[position] // blocks).reshape([-1 if axis == position else 1 for axis in range(len(dims))])
    return factor_of


def centred(stream_key, shape, scale, bound, cuts=(), kind=jnp.bfloat16):
    values = scale * jax.random.normal(stream_key, shape, jnp.float32)
    if cuts:
        values = values * levels(stream_key, shape, cuts, -0.22, 0.18)
    return jnp.clip(values, -bound, bound).astype(kind)


def setup_inputs(seed: int = 0) -> dict:
    keys = jax.random.split(jax.random.key(seed), 8)
    return {
        "sources": centred(keys[0], (POINTS, RHS), 1.0, 6.0, ((0, 32),)),
        "leaf_basis": centred(keys[1], (LEAVES, LEAF_PTS, RANK), LEAF_PTS ** -0.5, 0.375, ((0, 32),)),
        "transfer": centred(keys[2], (2, RANK, RANK), (3 * RANK // 2) ** -0.5, 0.625, (), jnp.float32),
        "coupling": centred(keys[3], (3, RANK, RANK), (2 * RANK) ** -0.5, 0.5, (), jnp.float32),
        "near_blocks": centred(keys[4], (LEAVES, NEAR, LEAF_PTS, LEAF_PTS), (NEAR * LEAF_PTS) ** -0.5, 0.1875, ((0, 32),)),
        "near_pattern": draw_near_pattern(jax.random.fold_in(keys[7], 71), 0),
        "far_pattern": touch_ends((jax.random.randint(keys[6], (FAR_ROWS, 3), 0, 3) < 2).astype(jnp.int32), jax.random.fold_in(keys[6], 1), 0, 1),
    }


PRECISE = lax.Precision.HIGHEST


def lift_up(level_vals, transfer):
    paired = level_vals.reshape(-1, 2, level_vals.shape[1], level_vals.shape[2])
    left_part = jnp.einsum('jk,pjr->pkr', transfer[0], paired[:, 0], precision=PRECISE)
    right_part = jnp.einsum('jk,pjr->pkr', transfer[1], paired[:, 1], precision=PRECISE)
    return left_part + right_part


def expand_down(parent_field, transfer):
    first_child = jnp.einsum('kj,pjr->pkr', transfer[0], parent_field, precision=PRECISE)
    second_child = jnp.einsum('kj,pjr->pkr', transfer[1], parent_field, precision=PRECISE)
    stacked = jnp.stack([first_child, second_child], 1)
    return stacked.reshape(-1, parent_field.shape[1], parent_field.shape[2])


def couple_level(level_vals, mask_rows, coupling):
    grouped = level_vals.reshape(-1, 4, level_vals.shape[1], level_vals.shape[2])
    summed = jnp.zeros(level_vals.shape, jnp.float32)
    for offset in range(1, 4):
        shifted = jnp.roll(grouped, -offset, axis=1).reshape(level_vals.shape)
        product_term = jnp.einsum('ab,nbr->nar', coupling[offset - 1], shifted, precision=PRECISE)
        weights = mask_rows[:, offset - 1:offset].astype(jnp.float32)[:, :, None]
        summed = summed + weights * product_term
    return summed


def reference(sources, leaf_basis, transfer, coupling, near_blocks, near_pattern, far_pattern):
    leaf_count = leaf_basis.shape[0]
    points = sources.reshape(leaf_count, LEAF_PTS, RHS).astype(jnp.float32)
    basis_wide = leaf_basis.astype(jnp.float32)
    moments = [jnp.einsum('lpk,lpr->lkr', basis_wide, points, precision=PRECISE)]
    while moments[-1].shape[0] > 4:
        moments.append(lift_up(moments[-1], transfer))
    locals_list = []
    row_start = 0
    for level_vals in moments:
        cluster_count = level_vals.shape[0]
        mask_rows = far_pattern[row_start:row_start + cluster_count]
        locals_list.append(couple_level(level_vals, mask_rows, coupling))
        row_start = row_start + cluster_count
    field_down = locals_list[-1]
    for level_id in range(len(moments) - 2, -1, -1):
        field_down = locals_list[level_id] + expand_down(field_down, transfer)
    far_part = jnp.einsum('lpk,lkr->lpr', basis_wide, field_down, precision=PRECISE)
    device_total = leaf_count // LEAF_DEV
    blocks_grouped = near_blocks.reshape(device_total, LEAF_DEV, NEAR, LEAF_PTS, LEAF_PTS)
    pattern_grouped = near_pattern.reshape(device_total, LEAF_DEV, NEAR)

    def near_one(inputs):
        blocks_here, pattern_here = inputs
        gathered = points[pattern_here]
        return jnp.einsum('lsab,lsbr->lar', blocks_here.astype(jnp.float32), gathered, precision=PRECISE)

    near_part = lax.map(near_one, (blocks_grouped, pattern_grouped)).reshape(leaf_count, LEAF_PTS, RHS)
    return (far_part + near_part).reshape(leaf_count * LEAF_PTS, RHS).astype(jnp.bfloat16)
```

```python
import functools

import jax
import jax.numpy as jnp
from jax import lax
from jax.experimental import pallas as pl
from jax.experimental.pallas import tpu as pltpu
from jax.sharding import PartitionSpec as P

BF = jnp.bfloat16
F32 = jnp.float32
MESH = pl.DeviceIdType.MESH


def halves(x):
    hi = x.astype(BF)
    return hi, (x - hi.astype(F32)).astype(BF)


def split(x):
    return jnp.concatenate(halves(x), axis=1)


def nt(a, b):
    return lax.dot_general(a, b, (((1,), (1,)), ((), ())), preferred_element_type=F32)


def nn(a, b):
    return jnp.dot(a, b, preferred_element_type=F32)


def fold(y, width):
    return y[:, :width] + y[:, width:]


def kernel(
    cfg, src, basis, transfer, coupling, blocks, near_pat, far_pat, out,
    buf, bas, nb, buf_a, pair2, buf4, buf5, buf6, wdown,
    load_sem, nb_sem, halo_send, halo_recv, a_send, a_recv, p_send, p_recv,
    b_send, b_recv, q_send, q_recv,
):
    sub, devices, leaf_dev, near = cfg
    rank = basis.shape[1]
    rhs = src.shape[0]
    points = basis.shape[2]
    block = 2 * sub
    block_count = devices // block
    me = lax.axis_index("leaf") * sub + lax.axis_index("sub")
    mine = lax.rem(me, block)
    own_block = me // block

    def target(dev):
        return (dev // sub, lax.rem(dev, sub))

    loads = [
        pltpu.make_async_copy(
            src.at[:, pl.ds(points * leaf, points)], buf.at[2, leaf], load_sem.at[leaf]
        )
        for leaf in range(leaf_dev)
    ]
    base_load = pltpu.make_async_copy(basis, bas, load_sem.at[leaf_dev])
    for copy in loads:
        copy.start()
    base_load.start()
    near_loads = [
        pltpu.make_async_copy(blocks.at[leaf], nb.at[leaf], nb_sem.at[leaf])
        for leaf in range(leaf_dev)
    ]
    for copy in near_loads:
        copy.start()

    barrier = pltpu.get_barrier_semaphore()
    steps = (-sub, -1, 1, sub)

    def present(step):
        return me + step >= 0 if step < 0 else me + step < devices

    peers = []
    for k in range(1, block):
        peers.append(own_block * block + lax.rem(mine + k, block))
    for k in range(1, block_count):
        peers.append(lax.rem(own_block + k, block_count) * block + mine)
    for peer in peers:
        pl.semaphore_signal(barrier, inc=1, device_id=target(peer), device_id_type=MESH)
    expected = len(peers)
    for step in steps:
        outside = present(step) & (lax.rem(me + step + devices, devices) // block != own_block)
        expected = expected + jnp.where(outside, 1, 0)

        @pl.when(outside)
        def _(step=step):
            pl.semaphore_signal(barrier, inc=1, device_id=target(me + step), device_id_type=MESH)
    thi, tlo = [], []
    for side in range(2):
        hi, lo = halves(transfer[side])
        thi.append(hi)
        tlo.append(lo)
    up_rows = []
    for side in range(2):
        row = jnp.concatenate([thi[side], tlo[side]], axis=1)
        up_rows += [row, row]
    w_up = jnp.concatenate(up_rows, axis=0)
    for side in range(2):
        wdown[side] = jnp.concatenate(
            [
                jnp.concatenate([thi[side], thi[side]], axis=1),
                jnp.concatenate([tlo[side], tlo[side]], axis=1),
            ],
            axis=0,
        )
    c_hi, c_lo = [], []
    for offset in range(3):
        hi, lo = halves(coupling[offset])
        c_hi += [hi, hi]
        c_lo += [lo, lo]
    w_couple = jnp.concatenate(
        [jnp.concatenate(c_hi, axis=1), jnp.concatenate(c_lo, axis=1)], axis=0
    )

    def lift(rows):
        return split(fold(nn(rows, w_up), rank))

    def pairs(split_vals, count):
        top = [
            jnp.concatenate(
                [
                    split_vals[2 * p * rhs : (2 * p + 1) * rhs],
                    split_vals[(2 * p + 1) * rhs : (2 * p + 2) * rhs],
                ],
                axis=1,
            )
            for p in range(count)
        ]
        return top[0] if count == 1 else jnp.concatenate(top, axis=0)

    pl.semaphore_wait(barrier, expected)
    for number, step in enumerate(steps):
        @pl.when(present(step))
        def _(step=step, number=number):
            slot = len(steps) - number if number < 2 else 3 - number
            for leaf in range(leaf_dev):
                pltpu.make_async_remote_copy(
                    src_ref=src.at[:, pl.ds(points * leaf, points)],
                    dst_ref=buf.at[slot, leaf],
                    send_sem=halo_send.at[number],
                    recv_sem=halo_recv.at[3 - number],
                    device_id=target(me + step),
                    device_id_type=MESH,
                ).start()

    for copy in loads:
        copy.wait()
    base_load.wait()
    moment0 = jnp.concatenate(
        [nt(buf[2, leaf], bas[leaf]) for leaf in range(leaf_dev)], axis=0
    )
    levels = [split(moment0)]
    count = leaf_dev
    while count > 2:
        count //= 2
        levels.append(lift(pairs(levels[-1], count)))
    two = pairs(levels[-1], 1)
    pair2[0] = two

    def remote(source, dest, send, recv, dev):
        return pltpu.make_async_remote_copy(
            src_ref=source, dst_ref=dest, send_sem=send, recv_sem=recv,
            device_id=target(dev), device_id_type=MESH,
        )

    sibling = me + 1 - 2 * lax.rem(me, 2)
    pair_copy = remote(pair2.at[0], pair2.at[1], p_send.at[0], p_recv.at[0], sibling)
    pair_copy.start()
    buf_a[mine] = lift(two)
    a_copies = []
    for k in range(1, block):
        a_copies.append(
            remote(
                buf_a.at[mine], buf_a.at[mine], a_send.at[k], a_recv.at[k],
                own_block * block + lax.rem(mine + k, block),
            )
        )
    for copy in a_copies:
        copy.start()

    row_starts = [0]
    total = leaf_dev * devices
    size = total
    while size > 4:
        row_starts.append(row_starts[-1] + size)
        size //= 2

    def weight(offset, row):
        return jnp.full((rhs, 2 * rank), far_pat[offset, row].astype(F32), F32).astype(BF)

    def couple(groups, rows):
        stacked = [
            jnp.concatenate(
                [weight(offset, row) * members[offset] for offset in range(3)], axis=1
            )
            for members, row in zip(groups, rows)
        ]
        stacked = stacked[0] if len(stacked) == 1 else jnp.concatenate(stacked, axis=0)
        return fold(nt(stacked, w_couple), rank)

    locals_low = []
    level_id = 0
    while (leaf_dev >> level_id) >= 4:
        vals = levels[level_id]
        count = leaf_dev >> level_id
        parts = [vals[c * rhs : (c + 1) * rhs] for c in range(count)]
        groups = [
            [parts[c // 4 * 4 + (c + offset) % 4] for offset in range(1, 4)] for c in range(count)
        ]
        rows = [row_starts[level_id] + me * count + c for c in range(count)]
        locals_low.append(couple(groups, rows))
        level_id += 1
    for copy in near_loads:
        copy.wait()
    first = [nt(buf[2, leaf], nb[leaf, 0]) for leaf in range(leaf_dev)]

    pair_copy.wait()
    other = pair2[1]
    members2 = [
        two[:, : 2 * rank], two[:, 2 * rank :], other[:, : 2 * rank], other[:, 2 * rank :]
    ]
    locals_low.append(
        couple(
            [[members2[(c + offset) % 4] for offset in range(1, 4)] for c in range(2)],
            [row_starts[level_id] + me * 2 + c for c in range(2)],
        )
    )
    level_id += 1

    for k in range(1, block):
        source = lax.rem(mine - k + block, block)
        remote(
            buf_a.at[source], buf_a.at[source], a_send.at[k], a_recv.at[k], me ^ 1
        ).wait_recv()
    quarter = block // 2
    four = lift(
        jnp.concatenate(
            [jnp.concatenate([buf_a[2 * p], buf_a[2 * p + 1]], axis=1) for p in range(quarter)],
            axis=0,
        )
    )
    for p in range(quarter):
        buf4[p] = four[p * rhs : (p + 1) * rhs]
    five = lift(pairs(four, 2))
    for p in range(2):
        buf5[p] = five[p * rhs : (p + 1) * rhs]
    buf6[own_block] = lift(pairs(five, 1))
    partner_block = own_block + 1 - 2 * lax.rem(own_block, 2)
    q_copy = remote(
        buf5.at[pl.ds(0, 2)], buf5.at[pl.ds(2, 2)], q_send.at[0], q_recv.at[0],
        partner_block * block + mine,
    )
    b_copies = []
    for k in range(1, block_count):
        b_copies.append(
            remote(
                buf6.at[own_block], buf6.at[own_block], b_send.at[k], b_recv.at[k],
                lax.rem(own_block + k, block_count) * block + mine,
            )
        )
    for copy in b_copies:
        copy.start()
    q_copy.start()

    base = mine // sub * sub
    place = lax.rem(me, sub)
    groups = [[buf_a[base + lax.rem(place + offset, 4)] for offset in range(1, 4)]]
    rows = [row_starts[level_id] + me]
    place = mine // 2
    groups.append([buf4[lax.rem(place + offset, 4)] for offset in range(1, 4)])
    rows.append(row_starts[level_id + 1] + me // 2)
    both = couple(groups, rows)
    locals_high = [both[:rhs], both[rhs:]]

    for k in range(1, block_count):
        source = lax.rem(own_block - k + block_count, block_count)
        remote(
            buf6.at[source], buf6.at[source], b_send.at[k], b_recv.at[k], me ^ 1
        ).wait_recv()
    q_copy.wait()
    place = mine // sub
    groups = [[buf5[lax.rem(place + offset, 4)] for offset in range(1, 4)]]
    rows = [row_starts[level_id + 2] + me // 4]
    first_six = level_id + 3
    groups.append(
        [
            buf6[own_block // 4 * 4 + lax.rem(lax.rem(own_block, 4) + offset, 4)]
            for offset in range(1, 4)
        ]
    )
    rows.append(row_starts[first_six] + own_block)
    start, span, level = 0, block_count, first_six
    while span > 4:
        above = lift(
            jnp.concatenate(
                [
                    jnp.concatenate([buf6[start + 2 * p], buf6[start + 2 * p + 1]], axis=1)
                    for p in range(span // 2)
                ],
                axis=0,
            )
        )
        for p in range(span // 2):
            buf6[start + span + p] = above[p * rhs : (p + 1) * rhs]
        start, span, level = start + span, span // 2, level + 1
        own = own_block >> (level - first_six)
        groups.append(
            [
                buf6[start + own // 4 * 4 + lax.rem(lax.rem(own, 4) + offset, 4)]
                for offset in range(1, 4)
            ]
        )
        rows.append(row_starts[level] + own)
    top = couple(groups, rows)
    locals_high += [top[p * rhs : (p + 1) * rhs] for p in range(len(groups))]

    field = locals_high[-1]
    for step in range(len(locals_high) - 2, -1, -1):
        parity = lax.rem(me >> step, 2)
        field = locals_high[step] + fold(nt(split(field), wdown[parity]), rank)
    w_down = jnp.concatenate([wdown[0], wdown[1]], axis=0)
    count = 1
    for step in range(len(locals_low) - 1, -1, -1):
        both = nt(split(field), w_down)
        children = []
        for p in range(count):
            row = both[p * rhs : (p + 1) * rhs]
            children.append(fold(row[:, : 2 * rank], rank))
            children.append(fold(row[:, 2 * rank :], rank))
        field = locals_low[step] + jnp.concatenate(children, axis=0)
        count *= 2
    spread = split(field)
    partial = []
    for leaf in range(leaf_dev):
        doubled = jnp.concatenate([bas[leaf], bas[leaf]], axis=0)
        partial.append(first[leaf] + nn(spread[leaf * rhs : (leaf + 1) * rhs], doubled))

    for number, step in enumerate(steps):
        @pl.when(present(step))
        def _(number=number):
            slot = number if number < 2 else number + 1
            pltpu.make_async_copy(buf.at[slot], buf.at[slot], halo_recv.at[number]).wait()
    for leaf in range(leaf_dev):
        acc = partial[leaf]
        for s in range(1, near):
            index = near_pat[s, leaf]
            gap = index // leaf_dev - me
            place = jnp.where(
                gap == -sub, 0, jnp.where(gap == -1, 1, jnp.where(gap == 0, 2, jnp.where(gap == 1, 3, 4)))
            )
            acc = acc + nt(buf[place, lax.rem(index, leaf_dev)], nb[leaf, s])
        out[:, points * leaf : points * (leaf + 1)] = acc.astype(out.dtype)

    for number, step in enumerate(steps):
        @pl.when(present(step))
        def _(number=number):
            pltpu.make_async_copy(buf.at[2], buf.at[2], halo_send.at[number]).wait()
    for copy in a_copies + b_copies:
        copy.wait_send()


def shards(sizes, sources, leaf_basis, transfer, coupling, near_blocks, near_pattern, far_pattern):
    sub, devices = sizes
    leaf_dev, points, rank = leaf_basis.shape
    rhs = sources.shape[1]
    near = near_blocks.shape[1]
    block = 2 * sub
    block_count = devices // block
    vmem = pl.BlockSpec(memory_space=pltpu.VMEM)
    smem = pl.BlockSpec(memory_space=pltpu.SMEM)
    hbm = pl.BlockSpec(memory_space=pl.ANY)
    dma = pltpu.SemaphoreType.DMA
    result = pl.pallas_call(
        functools.partial(kernel, (sub, devices, leaf_dev, near)),
        out_shape=jax.ShapeDtypeStruct((rhs, leaf_dev * points), BF),
        in_specs=[hbm, hbm, vmem, vmem, hbm, smem, smem],
        out_specs=vmem,
        scratch_shapes=[
            pltpu.VMEM((5, leaf_dev, rhs, points), BF),
            pltpu.VMEM((leaf_dev, rank, points), BF),
            pltpu.VMEM((leaf_dev, near, points, points), BF),
            pltpu.VMEM((block, rhs, 2 * rank), BF),
            pltpu.VMEM((2, rhs, 4 * rank), BF),
            pltpu.VMEM((4, rhs, 2 * rank), BF),
            pltpu.VMEM((4, rhs, 2 * rank), BF),
            pltpu.VMEM((2 * block_count, rhs, 2 * rank), BF),
            pltpu.VMEM((2, 2 * rank, 2 * rank), BF),
            dma((leaf_dev + 1,)),
            dma((leaf_dev,)),
            dma((4,)),
            dma((4,)),
            dma((block,)),
            dma((block,)),
            dma((1,)),
            dma((1,)),
            dma((block_count,)),
            dma((block_count,)),
            dma((1,)),
            dma((1,)),
        ],
        compiler_params=pltpu.CompilerParams(collective_id=0, has_side_effects=True),
    )(
        sources.T,
        leaf_basis.transpose(0, 2, 1),
        transfer,
        coupling,
        near_blocks,
        near_pattern.T,
        far_pattern.T,
    )
    return result.T


def solution(mesh):
    placed = (
        P(("leaf", "sub"), None),
        P(("leaf", "sub"), None, None),
        P(),
        P(),
        P(("leaf", "sub"), None, None, None),
        P(("leaf", "sub"), None),
        P(),
    )
    sizes = (mesh.shape["sub"], mesh.shape["leaf"] * mesh.shape["sub"])
    return jax.shard_map(
        functools.partial(shards, sizes),
        mesh=mesh, in_specs=placed, out_specs=P(("leaf", "sub"), None), check_vma=False,
    )
```

```python
import functools

import jax
import jax.numpy as jnp
from jax import lax
from jax.experimental import pallas as pl
from jax.experimental.pallas import tpu as pltpu
from jax.sharding import PartitionSpec as P

BF = jnp.bfloat16
F32 = jnp.float32
MESH = pl.DeviceIdType.MESH


def halves(x):
    hi = x.astype(BF)
    return hi, (x - hi.astype(F32)).astype(BF)


def split(x):
    return jnp.concatenate(halves(x), axis=1)


def nt(a, b):
    return lax.dot_general(a, b, (((1,), (1,)), ((), ())), preferred_element_type=F32)


def nn(a, b):
    return jnp.dot(a, b, preferred_element_type=F32)


def fold(y, width):
    return y[:, :width] + y[:, width:]


def kernel(
    cfg, src, basis, transfer, coupling, blocks, near_pat, far_pat, out,
    buf, bas, nb, buf_a, pair2, buf4, buf5, buf6, wdown, wpath,
    load_sem, nb_sem, halo_send, near_recv, y_recv, z_recv, a_send, a_recv, p_send, p_recv,
    b_send, b_recv, q_send, q_recv,
):
    sub, devices, leaf_dev, near = cfg
    rank = basis.shape[1]
    rhs = src.shape[0]
    points = basis.shape[2]
    block = 2 * sub
    block_count = devices // block
    me = lax.axis_index("leaf") * sub + lax.axis_index("sub")
    mine = lax.rem(me, block)
    own_block = me // block
    place_sub = lax.rem(me, sub)
    upper = mine // sub

    def target(dev):
        return (dev // sub, lax.rem(dev, sub))

    def remote(source, dest, send, recv, dev):
        return pltpu.make_async_remote_copy(
            src_ref=source, dst_ref=dest, send_sem=send, recv_sem=recv,
            device_id=target(dev), device_id_type=MESH,
        )

    barrier = pltpu.get_barrier_semaphore()
    peers = []
    for k in range(1, block_count):
        peers.append(lax.rem(own_block + k, block_count) * block + mine)
    for k in range(1, block):
        peers.append(own_block * block + lax.rem(mine + k, block))
    for peer in peers:
        pl.semaphore_signal(barrier, inc=1, device_id=target(peer), device_id_type=MESH)

    loads = [
        pltpu.make_async_copy(
            src.at[:, pl.ds(points * leaf, points)], buf.at[2, leaf], load_sem.at[leaf]
        )
        for leaf in range(leaf_dev)
    ]
    base_load = pltpu.make_async_copy(basis, bas, load_sem.at[leaf_dev])
    base_load.start()
    for copy in loads:
        copy.start()
    near_loads = [
        pltpu.make_async_copy(blocks.at[leaf], nb.at[leaf], nb_sem.at[leaf])
        for leaf in range(leaf_dev)
    ]
    for copy in near_loads:
        copy.start()

    def doubled(parts):
        rows = []
        for part in parts:
            row = split(part)
            rows += [row, row]
        return jnp.concatenate(rows, axis=0)

    sides = [transfer[side] for side in range(2)]
    step_weight = jnp.concatenate([doubled([side]) for side in sides], axis=1)
    w_up = {2: doubled(sides)}
    paths = sides
    while len(paths) < max(leaf_dev, block):
        wide = nn(split(jnp.concatenate(paths, axis=0)), step_weight)
        longer = jnp.concatenate(
            [fold(wide[:, : 2 * rank], rank), fold(wide[:, 2 * rank :], rank)], axis=0
        )
        paths = [longer[p * rank : (p + 1) * rank] for p in range(2 * len(paths))]
        w_up[len(paths)] = doubled(paths)

    def lift(parts, span):
        rows = [
            jnp.concatenate(parts[p * span : (p + 1) * span], axis=1)
            for p in range(len(parts) // span)
        ]
        rows = rows[0] if len(rows) == 1 else jnp.concatenate(rows, axis=0)
        lifted = split(fold(nn(rows, w_up[span]), rank))
        return [lifted[p * rhs : (p + 1) * rhs] for p in range(len(parts) // span)]

    base_load.wait()
    moment0 = []
    for leaf in range(leaf_dev):
        loads[leaf].wait()
        moment0.append(split(nt(buf[2, leaf], bas[leaf])))
    buf_a[mine] = lift(moment0, leaf_dev)[0]
    two = lift(moment0, leaf_dev // 2)
    pair2[0, 0] = two[0]
    pair2[0, 1] = two[1]

    pl.semaphore_wait(barrier, len(peers))
    a_copies = []
    for k in range(block - 1, 0, -1):
        a_copies.append(
            remote(
                buf_a.at[mine], buf_a.at[mine], a_send.at[k], a_recv.at[k],
                own_block * block + lax.rem(mine + k, block),
            )
        )
    for copy in a_copies:
        copy.start()
    pair_copy = remote(
        pair2.at[0], pair2.at[1], p_send.at[0], p_recv.at[0], me + 1 - 2 * lax.rem(me, 2)
    )
    pair_copy.start()

    y_slot = 4 - 4 * upper
    z_slot = 4 * upper
    across = me + sub - 2 * sub * upper
    for leaf in range(leaf_dev):
        remote(
            src.at[:, pl.ds(points * leaf, points)], buf.at[z_slot, leaf],
            halo_send.at[0], y_recv.at[leaf], across,
        ).start()
    for number, step in enumerate((1, -1)):
        @pl.when(place_sub < sub - 1 if step > 0 else place_sub > 0)
        def _(number=number, step=step):
            for leaf in range(leaf_dev):
                remote(
                    src.at[:, pl.ds(points * leaf, points)], buf.at[2 - step, leaf],
                    halo_send.at[1 + number], near_recv.at[number], me + step,
                ).start()

    z_step = block - 2 * block * upper
    z_target = me + z_step
    z_send = (z_target >= 0) & (z_target < devices)
    z_have = (me - z_step >= 0) & (me - z_step < devices)
    first_turn = ((upper == 0) & (place_sub == 0)) | ((upper == 1) & (place_sub == sub - 1))
    second_turn = z_have & (
        ((upper == 0) & (place_sub == sub - 1)) | ((upper == 1) & (place_sub == 0))
    )

    def turn(slot, leaf):
        @pl.when(place_sub == 0)
        def _():
            remote(
                buf.at[slot, leaf], buf.at[3, leaf],
                halo_send.at[4], near_recv.at[1], me + sub - 1,
            ).start()

        @pl.when(place_sub == sub - 1)
        def _():
            remote(
                buf.at[slot, leaf], buf.at[1, leaf],
                halo_send.at[4], near_recv.at[0], me - sub + 1,
            ).start()

    def relay_first(leaf):
        remote(
            buf.at[y_slot, leaf], buf.at[y_slot, leaf], halo_send.at[0], y_recv.at[leaf], across
        ).wait_recv()

        @pl.when(z_send)
        def _():
            remote(
                buf.at[y_slot, leaf], buf.at[z_slot, leaf],
                halo_send.at[3], z_recv.at[leaf], z_target,
            ).start()

        @pl.when(first_turn)
        def _():
            turn(y_slot, leaf)

    def z_wait(leaf):
        remote(
            buf.at[z_slot, leaf], buf.at[z_slot, leaf], halo_send.at[3], z_recv.at[leaf], across
        ).wait_recv()

    def relay_second(leaf):
        @pl.when(second_turn)
        def _():
            z_wait(leaf)
            turn(z_slot, leaf)

    row_starts = [0]
    size = leaf_dev * devices
    while size > 4:
        row_starts.append(row_starts[-1] + size)
        size //= 2

    def weight(offset, row):
        return jnp.full((rhs, 2 * rank), far_pat[offset, row].astype(F32), F32).astype(BF)

    c_hi, c_lo = [], []
    for offset in range(3):
        hi, lo = halves(coupling[offset])
        c_hi += [hi, hi]
        c_lo += [lo, lo]
    w_couple = jnp.concatenate(
        [jnp.concatenate(c_hi, axis=1), jnp.concatenate(c_lo, axis=1)], axis=0
    )

    def couple(groups, rows):
        stacked = [
            jnp.concatenate(
                [weight(offset, row) * members[offset] for offset in range(3)], axis=1
            )
            for members, row in zip(groups, rows)
        ]
        stacked = stacked[0] if len(stacked) == 1 else jnp.concatenate(stacked, axis=0)
        return fold(nt(stacked, w_couple), rank)

    for side in range(2):
        hi, lo = halves(sides[side])
        wdown[side] = jnp.concatenate(
            [jnp.concatenate([hi, hi], axis=1), jnp.concatenate([lo, lo], axis=1)], axis=0
        )
    w_down = jnp.concatenate([wdown[0], wdown[1]], axis=0)

    def descend(field, step):
        return fold(nt(split(field), wdown[lax.rem(me >> step, 2)]), rank)

    def fan_out(field, rows):
        both = nt(split(field), w_down)
        children = []
        for p in range(field.shape[0] // rows):
            row = both[p * rows : (p + 1) * rows]
            children.append(fold(row[:, : 2 * rank], rank))
            children.append(fold(row[:, 2 * rank :], rank))
        return jnp.concatenate(children, axis=0)

    low_levels = leaf_dev.bit_length() - 1
    top_count = len(row_starts) - low_levels - 2
    eye = (
        lax.broadcasted_iota(jnp.int32, (rank, rank), 0)
        == lax.broadcasted_iota(jnp.int32, (rank, rank), 1)
    ).astype(F32)
    chain = eye
    for step in range(top_count, -1, -1):
        if step <= 1:
            chain = descend(chain, step)
        elif step < top_count + 1:
            chain = jnp.concatenate([descend(chain, step), eye], axis=0)
    for _ in range(low_levels):
        chain = fan_out(chain, top_count * rank)
    for leaf in range(leaf_dev):
        for number in range(top_count):
            begin = (leaf * top_count + number) * rank
            piece = split(chain[begin : begin + rank])
            for half in range(2):
                wpath[
                    (2 * number + half) * rank : (2 * number + half + 1) * rank,
                    2 * rank * leaf : 2 * rank * (leaf + 1),
                ] = piece

    locals_low = []
    level_vals, level_id = moment0, 0
    while (leaf_dev >> level_id) >= 4:
        if level_id:
            level_vals = lift(level_vals, 2)
        count = leaf_dev >> level_id
        locals_low.append(
            couple(
                [
                    [level_vals[c // 4 * 4 + (c + offset) % 4] for offset in range(1, 4)]
                    for c in range(count)
                ],
                [row_starts[level_id] + me * count + c for c in range(count)],
            )
        )
        level_id += 1

    for k in range(block - 1, 0, -1):
        source = lax.rem(mine - k + block, block)
        remote(
            buf_a.at[source], buf_a.at[source], a_send.at[k], a_recv.at[k], me ^ 1
        ).wait_recv()
    eight = [buf_a[p] for p in range(block)]
    buf6[own_block] = lift(eight, block)[0]
    b_copies = []
    for k in range(block_count - 1, 0, -1):
        b_copies.append(
            remote(
                buf6.at[own_block], buf6.at[own_block], b_send.at[k], b_recv.at[k],
                lax.rem(own_block + k, block_count) * block + mine,
            )
        )
    for copy in b_copies:
        copy.start()
    five = lift(eight, block // 2)
    for p in range(2):
        buf5[p] = five[p]
    q_copy = remote(
        buf5.at[pl.ds(0, 2)], buf5.at[pl.ds(2, 2)], q_send.at[0], q_recv.at[0],
        (own_block + 1 - 2 * lax.rem(own_block, 2)) * block + mine,
    )
    q_copy.start()
    relay_first(0)
    relay_first(1)
    for p, part in enumerate(lift(eight, 2)):
        buf4[p] = part

    pair_copy.wait()
    members2 = two + [pair2[1, 0], pair2[1, 1]]
    groups = [[members2[(c + offset) % 4] for offset in range(1, 4)] for c in range(2)]
    rows = [row_starts[level_id] + me * 2 + c for c in range(2)]
    level_id += 1
    groups.append(
        [buf_a[upper * sub + lax.rem(place_sub + offset, 4)] for offset in range(1, 4)]
    )
    rows.append(row_starts[level_id] + me)
    groups.append([buf4[lax.rem(mine // 2 + offset, 4)] for offset in range(1, 4)])
    rows.append(row_starts[level_id + 1] + me // 2)
    relay_first(2)
    middle = couple(groups, rows)
    locals_low.append(middle[: 2 * rhs])
    relay_first(3)
    field = middle[2 * rhs : 3 * rhs] + descend(middle[3 * rhs :], 0)
    for step in range(len(locals_low) - 1, -1, -1):
        field = locals_low[step] + fan_out(field, rhs)
    relay_first(4)

    for copy in near_loads:
        copy.wait()
    first = [nt(buf[2, leaf], nb[leaf, 0]) for leaf in range(leaf_dev)]
    for leaf in range(5, leaf_dev):
        relay_first(leaf)
    for leaf in range(leaf_dev):
        relay_second(leaf)

    for k in range(block_count - 1, 0, -1):
        source = lax.rem(own_block - k + block_count, block_count)
        remote(
            buf6.at[source], buf6.at[source], b_send.at[k], b_recv.at[k], me ^ 1
        ).wait_recv()
    q_copy.wait()
    groups = [[buf5[lax.rem(upper + offset, 4)] for offset in range(1, 4)]]
    rows = [row_starts[level_id + 2] + me // sub]
    first_six = level_id + 3
    start, span, level = 0, block_count, first_six
    while True:
        own = own_block >> (level - first_six)
        groups.append(
            [
                buf6[start + own // 4 * 4 + lax.rem(lax.rem(own, 4) + offset, 4)]
                for offset in range(1, 4)
            ]
        )
        rows.append(row_starts[level] + own)
        if span <= 4:
            break
        for p, part in enumerate(lift([buf6[start + p] for p in range(span)], 2)):
            buf6[start + span + p] = part
        start, span, level = start + span, span // 2, level + 1
    groups, rows = groups[::-1], rows[::-1]
    top = split(couple(groups, rows))
    top = jnp.concatenate([top[p * rhs : (p + 1) * rhs] for p in range(top_count)], axis=1)
    spread = nn(top, wpath[...])
    partial = []
    for leaf in range(leaf_dev):
        whole = split(
            field[leaf * rhs : (leaf + 1) * rhs]
            + fold(spread[:, 2 * rank * leaf : 2 * rank * (leaf + 1)], rank)
        )
        twice = jnp.concatenate([bas[leaf], bas[leaf]], axis=0)
        partial.append(first[leaf] + nn(whole, twice))

    @pl.when(z_have & jnp.logical_not(second_turn))
    def _():
        for leaf in range(leaf_dev):
            z_wait(leaf)

    for number, step in enumerate((-1, 1)):
        @pl.when(me > 0 if step < 0 else me < devices - 1)
        def _(number=number, step=step):
            pltpu.make_async_copy(buf.at[2 + step], buf.at[2 + step], near_recv.at[number]).wait()
    for leaf in range(leaf_dev):
        acc = partial[leaf]
        for s in range(1, near):
            index = near_pat[s, leaf]
            gap = index // leaf_dev - me
            place = jnp.where(
                gap == -sub, 0, jnp.where(gap == -1, 1, jnp.where(gap == 0, 2, jnp.where(gap == 1, 3, 4)))
            )
            acc = acc + nt(buf[place, lax.rem(index, leaf_dev)], nb[leaf, s])
        out[:, points * leaf : points * (leaf + 1)] = acc.astype(out.dtype)

    sent = (
        me >= 0, place_sub < sub - 1, place_sub > 0, z_send, first_turn | second_turn,
    )
    for number, condition in enumerate(sent):
        @pl.when(condition)
        def _(number=number):
            pltpu.make_async_copy(buf.at[2], buf.at[2], halo_send.at[number]).wait()
    for copy in a_copies + b_copies:
        copy.wait_send()


def shards(sizes, sources, leaf_basis, transfer, coupling, near_blocks, near_pattern, far_pattern):
    sub, devices = sizes
    leaf_dev, points, rank = leaf_basis.shape
    rhs = sources.shape[1]
    near = near_blocks.shape[1]
    block = 2 * sub
    block_count = devices // block
    top_count = block_count.bit_length() - 1
    vmem = pl.BlockSpec(memory_space=pltpu.VMEM)
    smem = pl.BlockSpec(memory_space=pltpu.SMEM)
    hbm = pl.BlockSpec(memory_space=pl.ANY)
    dma = pltpu.SemaphoreType.DMA
    result = pl.pallas_call(
        functools.partial(kernel, (sub, devices, leaf_dev, near)),
        out_shape=jax.ShapeDtypeStruct((rhs, leaf_dev * points), BF),
        in_specs=[hbm, hbm, vmem, vmem, hbm, smem, smem],
        out_specs=vmem,
        scratch_shapes=[
            pltpu.VMEM((5, leaf_dev, rhs, points), BF),
            pltpu.VMEM((leaf_dev, rank, points), BF),
            pltpu.VMEM((leaf_dev, near, points, points), BF),
            pltpu.VMEM((block, rhs, 2 * rank), BF),
            pltpu.VMEM((2, 2, rhs, 2 * rank), BF),
            pltpu.VMEM((4, rhs, 2 * rank), BF),
            pltpu.VMEM((4, rhs, 2 * rank), BF),
            pltpu.VMEM((2 * block_count, rhs, 2 * rank), BF),
            pltpu.VMEM((2, 2 * rank, 2 * rank), BF),
            pltpu.VMEM((2 * top_count * rank, 2 * rank * leaf_dev), BF),
            dma((leaf_dev + 1,)),
            dma((leaf_dev,)),
            dma((5,)),
            dma((2,)),
            dma((leaf_dev,)),
            dma((leaf_dev,)),
            dma((block,)),
            dma((block,)),
            dma((1,)),
            dma((1,)),
            dma((block_count,)),
            dma((block_count,)),
            dma((1,)),
            dma((1,)),
        ],
        compiler_params=pltpu.CompilerParams(collective_id=0, has_side_effects=True),
    )(
        sources.T,
        leaf_basis.transpose(0, 2, 1),
        transfer,
        coupling,
        near_blocks,
        near_pattern.T,
        far_pattern.T,
    )
    return result.T


def solution(mesh):
    placed = (
        P(("leaf", "sub"), None),
        P(("leaf", "sub"), None, None),
        P(),
        P(),
        P(("leaf", "sub"), None, None, None),
        P(("leaf", "sub"), None),
        P(),
    )
    sizes = (mesh.shape["sub"], mesh.shape["leaf"] * mesh.shape["sub"])
    return jax.shard_map(
        functools.partial(shards, sizes),
        mesh=mesh, in_specs=placed, out_specs=P(("leaf", "sub"), None), check_vma=False,
    )
```

```python
import functools

import jax
import jax.numpy as jnp
from jax import lax
from jax.experimental import pallas as pl
from jax.experimental.pallas import tpu as pltpu
from jax.sharding import PartitionSpec as P

BF = jnp.bfloat16
F32 = jnp.float32
MESH = pl.DeviceIdType.MESH


def halves(x):
    hi = x.astype(BF)
    return hi, (x - hi.astype(F32)).astype(BF)


def split(x):
    return jnp.concatenate(halves(x), axis=1)


def nt(a, b):
    return lax.dot_general(a, b, (((1,), (1,)), ((), ())), preferred_element_type=F32)


def nn(a, b):
    return jnp.dot(a, b, preferred_element_type=F32)


def fold(y, width):
    return y[:, :width] + y[:, width:]


def kernel(
    cfg, src, basis, transfer, coupling, blocks, near_pat, far_pat, out,
    buf, bas, nb, buf_a, pair2, buf4, buf5, buf6, wdown, wpath,
    load_sem, nb_sem, halo_send, near_recv, y_recv, z_recv, a_send, a_recv, p_send, p_recv,
    b_send, b_recv, q_send, q_recv,
):
    sub, devices, leaf_dev, near = cfg
    rank = basis.shape[1]
    rhs = src.shape[0]
    points = basis.shape[2]
    block = 2 * sub
    block_count = devices // block
    me = lax.axis_index("leaf") * sub + lax.axis_index("sub")
    mine = lax.rem(me, block)
    own_block = me // block
    place_sub = lax.rem(me, sub)
    upper = mine // sub

    def target(dev):
        return (dev // sub, lax.rem(dev, sub))

    def remote(source, dest, send, recv, dev):
        return pltpu.make_async_remote_copy(
            src_ref=source, dst_ref=dest, send_sem=send, recv_sem=recv,
            device_id=target(dev), device_id_type=MESH,
        )

    barrier = pltpu.get_barrier_semaphore()
    peers = []
    for k in range(1, block_count):
        peers.append(lax.rem(own_block + k, block_count) * block + mine)
    for k in range(1, block):
        peers.append(own_block * block + lax.rem(mine + k, block))
    for peer in peers:
        pl.semaphore_signal(barrier, inc=1, device_id=target(peer), device_id_type=MESH)

    loads = [
        pltpu.make_async_copy(
            src.at[:, pl.ds(points * leaf, points)], buf.at[2, leaf], load_sem.at[leaf]
        )
        for leaf in range(leaf_dev)
    ]
    base_load = pltpu.make_async_copy(basis, bas, load_sem.at[leaf_dev])
    base_load.start()
    for copy in loads:
        copy.start()
    near_loads = [
        pltpu.make_async_copy(blocks.at[leaf], nb.at[leaf], nb_sem.at[leaf])
        for leaf in range(leaf_dev)
    ]
    for copy in near_loads:
        copy.start()

    def doubled(parts):
        rows = []
        for part in parts:
            row = split(part)
            rows += [row, row]
        return jnp.concatenate(rows, axis=0)

    sides = [transfer[side] for side in range(2)]
    step_weight = jnp.concatenate([doubled([side]) for side in sides], axis=1)
    w_up = {2: doubled(sides)}
    paths = sides
    while len(paths) < max(leaf_dev, block):
        wide = nn(split(jnp.concatenate(paths, axis=0)), step_weight)
        longer = jnp.concatenate(
            [fold(wide[:, : 2 * rank], rank), fold(wide[:, 2 * rank :], rank)], axis=0
        )
        paths = [longer[p * rank : (p + 1) * rank] for p in range(2 * len(paths))]
        w_up[len(paths)] = doubled(paths)

    def lift(parts, span):
        rows = [
            jnp.concatenate(parts[p * span : (p + 1) * span], axis=1)
            for p in range(len(parts) // span)
        ]
        rows = rows[0] if len(rows) == 1 else jnp.concatenate(rows, axis=0)
        lifted = split(fold(nn(rows, w_up[span]), rank))
        return [lifted[p * rhs : (p + 1) * rhs] for p in range(len(parts) // span)]

    base_load.wait()
    for copy in loads:
        copy.wait()
    moment0 = [split(nt(buf[2, leaf], bas[leaf])) for leaf in range(leaf_dev)]
    buf_a[mine] = lift(moment0, leaf_dev)[0]
    two = lift(moment0, leaf_dev // 2)
    pair2[0, 0] = two[0]
    pair2[0, 1] = two[1]

    pl.semaphore_wait(barrier, len(peers))
    a_copies = []
    for k in range(block - 1, 0, -1):
        a_copies.append(
            remote(
                buf_a.at[mine], buf_a.at[mine], a_send.at[k], a_recv.at[k],
                own_block * block + lax.rem(mine + k, block),
            )
        )
    for copy in a_copies:
        copy.start()
    pair_copy = remote(
        pair2.at[0], pair2.at[1], p_send.at[0], p_recv.at[0], me + 1 - 2 * lax.rem(me, 2)
    )
    pair_copy.start()

    y_slot = 4 - 4 * upper
    z_slot = 4 * upper
    across = me + sub - 2 * sub * upper

    def send_across():
        for leaf in range(leaf_dev):
            remote(
                src.at[:, pl.ds(points * leaf, points)], buf.at[z_slot, leaf],
                halo_send.at[0], y_recv.at[leaf], across,
            ).start()

    outer = (place_sub == 0) | (place_sub == sub - 1)
    pl.when(outer)(send_across)
    for number, step in enumerate((1, -1)):
        @pl.when(place_sub < sub - 1 if step > 0 else place_sub > 0)
        def _(number=number, step=step):
            for leaf in range(leaf_dev):
                remote(
                    src.at[:, pl.ds(points * leaf, points)], buf.at[2 - step, leaf],
                    halo_send.at[1 + number], near_recv.at[number], me + step,
                ).start()

    z_step = block - 2 * block * upper
    z_target = me + z_step
    z_send = (z_target >= 0) & (z_target < devices)
    z_have = (me - z_step >= 0) & (me - z_step < devices)
    first_turn = ((upper == 0) & (place_sub == 0)) | ((upper == 1) & (place_sub == sub - 1))
    second_turn = z_have & (
        ((upper == 0) & (place_sub == sub - 1)) | ((upper == 1) & (place_sub == 0))
    )

    def turn(slot, leaf):
        @pl.when(place_sub == 0)
        def _():
            remote(
                buf.at[slot, leaf], buf.at[3, leaf],
                halo_send.at[4], near_recv.at[1], me + sub - 1,
            ).start()

        @pl.when(place_sub == sub - 1)
        def _():
            remote(
                buf.at[slot, leaf], buf.at[1, leaf],
                halo_send.at[4], near_recv.at[0], me - sub + 1,
            ).start()

    def relay_first(leaf):
        remote(
            buf.at[y_slot, leaf], buf.at[y_slot, leaf], halo_send.at[0], y_recv.at[leaf], across
        ).wait_recv()

        @pl.when(z_send)
        def _():
            remote(
                buf.at[y_slot, leaf], buf.at[z_slot, leaf],
                halo_send.at[3], z_recv.at[leaf], z_target,
            ).start()

        @pl.when(first_turn)
        def _():
            turn(y_slot, leaf)

    def z_wait(leaf):
        remote(
            buf.at[z_slot, leaf], buf.at[z_slot, leaf], halo_send.at[3], z_recv.at[leaf], across
        ).wait_recv()

    def relay_second(leaf):
        @pl.when(second_turn)
        def _():
            z_wait(leaf)
            turn(z_slot, leaf)

    row_starts = [0]
    size = leaf_dev * devices
    while size > 4:
        row_starts.append(row_starts[-1] + size)
        size //= 2

    def weight(offset, row):
        return jnp.full((rhs, 2 * rank), far_pat[offset, row].astype(F32), F32).astype(BF)

    c_hi, c_lo = [], []
    for offset in range(3):
        hi, lo = halves(coupling[offset])
        c_hi += [hi, hi]
        c_lo += [lo, lo]
    w_couple = jnp.concatenate(
        [jnp.concatenate(c_hi, axis=1), jnp.concatenate(c_lo, axis=1)], axis=0
    )

    def couple(groups, rows):
        stacked = [
            jnp.concatenate(
                [weight(offset, row) * members[offset] for offset in range(3)], axis=1
            )
            for members, row in zip(groups, rows)
        ]
        stacked = stacked[0] if len(stacked) == 1 else jnp.concatenate(stacked, axis=0)
        return fold(nt(stacked, w_couple), rank)

    for side in range(2):
        hi, lo = halves(sides[side])
        wdown[side] = jnp.concatenate(
            [jnp.concatenate([hi, hi], axis=1), jnp.concatenate([lo, lo], axis=1)], axis=0
        )
    w_down = jnp.concatenate([wdown[0], wdown[1]], axis=0)

    def descend(field, step):
        return fold(nt(split(field), wdown[lax.rem(me >> step, 2)]), rank)

    def fan_out(field, rows):
        both = nt(split(field), w_down)
        children = []
        for p in range(field.shape[0] // rows):
            row = both[p * rows : (p + 1) * rows]
            children.append(fold(row[:, : 2 * rank], rank))
            children.append(fold(row[:, 2 * rank :], rank))
        return jnp.concatenate(children, axis=0)

    low_levels = leaf_dev.bit_length() - 1
    top_count = len(row_starts) - low_levels - 2
    eye = (
        lax.broadcasted_iota(jnp.int32, (rank, rank), 0)
        == lax.broadcasted_iota(jnp.int32, (rank, rank), 1)
    ).astype(F32)
    chain = eye
    for step in range(top_count, -1, -1):
        if step <= 1:
            chain = descend(chain, step)
        elif step < top_count + 1:
            chain = jnp.concatenate([descend(chain, step), eye], axis=0)
    for _ in range(low_levels):
        chain = fan_out(chain, top_count * rank)
    for leaf in range(leaf_dev):
        for number in range(top_count):
            begin = (leaf * top_count + number) * rank
            piece = split(chain[begin : begin + rank])
            for half in range(2):
                wpath[
                    (2 * number + half) * rank : (2 * number + half + 1) * rank,
                    2 * rank * leaf : 2 * rank * (leaf + 1),
                ] = piece

    locals_low = []
    level_vals, level_id = moment0, 0
    while (leaf_dev >> level_id) >= 4:
        if level_id:
            level_vals = lift(level_vals, 2)
        count = leaf_dev >> level_id
        locals_low.append(
            couple(
                [
                    [level_vals[c // 4 * 4 + (c + offset) % 4] for offset in range(1, 4)]
                    for c in range(count)
                ],
                [row_starts[level_id] + me * count + c for c in range(count)],
            )
        )
        level_id += 1

    pl.when(jnp.logical_not(outer))(send_across)

    for k in range(block - 1, 0, -1):
        source = lax.rem(mine - k + block, block)
        remote(
            buf_a.at[source], buf_a.at[source], a_send.at[k], a_recv.at[k], me ^ 1
        ).wait_recv()
    eight = [buf_a[p] for p in range(block)]
    buf6[own_block] = lift(eight, block)[0]
    b_copies = []
    for k in range(block_count - 1, 0, -1):
        b_copies.append(
            remote(
                buf6.at[own_block], buf6.at[own_block], b_send.at[k], b_recv.at[k],
                lax.rem(own_block + k, block_count) * block + mine,
            )
        )
    for copy in b_copies:
        copy.start()
    five = lift(eight, block // 2)
    for p in range(2):
        buf5[p] = five[p]
    q_copy = remote(
        buf5.at[pl.ds(0, 2)], buf5.at[pl.ds(2, 2)], q_send.at[0], q_recv.at[0],
        (own_block + 1 - 2 * lax.rem(own_block, 2)) * block + mine,
    )
    q_copy.start()
    relay_first(0)
    relay_first(1)
    for p, part in enumerate(lift(eight, 2)):
        buf4[p] = part

    pair_copy.wait()
    members2 = two + [pair2[1, 0], pair2[1, 1]]
    groups = [[members2[(c + offset) % 4] for offset in range(1, 4)] for c in range(2)]
    rows = [row_starts[level_id] + me * 2 + c for c in range(2)]
    level_id += 1
    groups.append(
        [buf_a[upper * sub + lax.rem(place_sub + offset, 4)] for offset in range(1, 4)]
    )
    rows.append(row_starts[level_id] + me)
    groups.append([buf4[lax.rem(mine // 2 + offset, 4)] for offset in range(1, 4)])
    rows.append(row_starts[level_id + 1] + me // 2)
    relay_first(2)
    middle = couple(groups, rows)
    locals_low.append(middle[: 2 * rhs])
    relay_first(3)
    field = middle[2 * rhs : 3 * rhs] + descend(middle[3 * rhs :], 0)
    for step in range(len(locals_low) - 1, -1, -1):
        field = locals_low[step] + fan_out(field, rhs)
    relay_first(4)

    for copy in near_loads:
        copy.wait()
    first = [nt(buf[2, leaf], nb[leaf, 0]) for leaf in range(leaf_dev)]
    for leaf in range(5, leaf_dev):
        relay_first(leaf)
    for leaf in range(leaf_dev):
        relay_second(leaf)

    for k in range(block_count - 1, 0, -1):
        source = lax.rem(own_block - k + block_count, block_count)
        remote(
            buf6.at[source], buf6.at[source], b_send.at[k], b_recv.at[k], me ^ 1
        ).wait_recv()
    q_copy.wait()
    groups = [[buf5[lax.rem(upper + offset, 4)] for offset in range(1, 4)]]
    rows = [row_starts[level_id + 2] + me // sub]
    first_six = level_id + 3
    start, span, level = 0, block_count, first_six
    while True:
        own = own_block >> (level - first_six)
        groups.append(
            [
                buf6[start + own // 4 * 4 + lax.rem(lax.rem(own, 4) + offset, 4)]
                for offset in range(1, 4)
            ]
        )
        rows.append(row_starts[level] + own)
        if span <= 4:
            break
        for p, part in enumerate(lift([buf6[start + p] for p in range(span)], 2)):
            buf6[start + span + p] = part
        start, span, level = start + span, span // 2, level + 1
    groups, rows = groups[::-1], rows[::-1]
    top = split(couple(groups, rows))
    top = jnp.concatenate([top[p * rhs : (p + 1) * rhs] for p in range(top_count)], axis=1)
    spread = nn(top, wpath[...])
    partial = []
    for leaf in range(leaf_dev):
        whole = split(
            field[leaf * rhs : (leaf + 1) * rhs]
            + fold(spread[:, 2 * rank * leaf : 2 * rank * (leaf + 1)], rank)
        )
        twice = jnp.concatenate([bas[leaf], bas[leaf]], axis=0)
        partial.append(first[leaf] + nn(whole, twice))

    @pl.when(z_have & jnp.logical_not(second_turn))
    def _():
        for leaf in range(leaf_dev):
            z_wait(leaf)

    for number, step in enumerate((-1, 1)):
        @pl.when(me > 0 if step < 0 else me < devices - 1)
        def _(number=number, step=step):
            pltpu.make_async_copy(buf.at[2 + step], buf.at[2 + step], near_recv.at[number]).wait()
    for leaf in range(leaf_dev):
        acc = partial[leaf]
        for s in range(1, near):
            index = near_pat[s, leaf]
            gap = index // leaf_dev - me
            place = jnp.where(
                gap == -sub, 0, jnp.where(gap == -1, 1, jnp.where(gap == 0, 2, jnp.where(gap == 1, 3, 4)))
            )
            acc = acc + nt(buf[place, lax.rem(index, leaf_dev)], nb[leaf, s])
        out[:, points * leaf : points * (leaf + 1)] = acc.astype(out.dtype)

    sent = (
        me >= 0, place_sub < sub - 1, place_sub > 0, z_send, first_turn | second_turn,
    )
    for number, condition in enumerate(sent):
        @pl.when(condition)
        def _(number=number):
            pltpu.make_async_copy(buf.at[2], buf.at[2], halo_send.at[number]).wait()
    for copy in a_copies + b_copies:
        copy.wait_send()


def shards(sizes, sources, leaf_basis, transfer, coupling, near_blocks, near_pattern, far_pattern):
    sub, devices = sizes
    leaf_dev, points, rank = leaf_basis.shape
    rhs = sources.shape[1]
    near = near_blocks.shape[1]
    block = 2 * sub
    block_count = devices // block
    top_count = block_count.bit_length() - 1
    vmem = pl.BlockSpec(memory_space=pltpu.VMEM)
    smem = pl.BlockSpec(memory_space=pltpu.SMEM)
    hbm = pl.BlockSpec(memory_space=pl.ANY)
    dma = pltpu.SemaphoreType.DMA
    result = pl.pallas_call(
        functools.partial(kernel, (sub, devices, leaf_dev, near)),
        out_shape=pltpu.VMEM((rhs, leaf_dev * points), BF),
        in_specs=[hbm, hbm, vmem, vmem, hbm, smem, smem],
        out_specs=vmem,
        scratch_shapes=[
            pltpu.VMEM((5, leaf_dev, rhs, points), BF),
            pltpu.VMEM((leaf_dev, rank, points), BF),
            pltpu.VMEM((leaf_dev, near, points, points), BF),
            pltpu.VMEM((block, rhs, 2 * rank), BF),
            pltpu.VMEM((2, 2, rhs, 2 * rank), BF),
            pltpu.VMEM((4, rhs, 2 * rank), BF),
            pltpu.VMEM((4, rhs, 2 * rank), BF),
            pltpu.VMEM((2 * block_count, rhs, 2 * rank), BF),
            pltpu.VMEM((2, 2 * rank, 2 * rank), BF),
            pltpu.VMEM((2 * top_count * rank, 2 * rank * leaf_dev), BF),
            dma((leaf_dev + 1,)),
            dma((leaf_dev,)),
            dma((5,)),
            dma((2,)),
            dma((leaf_dev,)),
            dma((leaf_dev,)),
            dma((block,)),
            dma((block,)),
            dma((1,)),
            dma((1,)),
            dma((block_count,)),
            dma((block_count,)),
            dma((1,)),
            dma((1,)),
        ],
        compiler_params=pltpu.CompilerParams(collective_id=0, has_side_effects=True),
    )(
        sources.T,
        leaf_basis.transpose(0, 2, 1),
        transfer,
        coupling,
        near_blocks,
        near_pattern.T,
        far_pattern.T,
    )
    return result.T


def solution(mesh):
    placed = (
        P(("leaf", "sub"), None),
        P(("leaf", "sub"), None, None),
        P(),
        P(),
        P(("leaf", "sub"), None, None, None),
        P(("leaf", "sub"), None),
        P(),
    )
    sizes = (mesh.shape["sub"], mesh.shape["leaf"] * mesh.shape["sub"])
    return jax.shard_map(
        functools.partial(shards, sizes),
        mesh=mesh, in_specs=placed, out_specs=P(("leaf", "sub"), None), check_vma=False,
    )
```

```python
import functools

import jax
import jax.numpy as jnp
from jax import lax
from jax.experimental import pallas as pl
from jax.experimental.pallas import tpu as pltpu
from jax.sharding import PartitionSpec as P

BF = jnp.bfloat16
F32 = jnp.float32
MESH = pl.DeviceIdType.MESH


def halves(x):
    hi = x.astype(BF)
    return hi, (x - hi.astype(F32)).astype(BF)


def split(x):
    return jnp.concatenate(halves(x), axis=1)


def nt(a, b):
    return lax.dot_general(a, b, (((1,), (1,)), ((), ())), preferred_element_type=F32)


def nn(a, b):
    return jnp.dot(a, b, preferred_element_type=F32)


def fold(y, width):
    return y[:, :width] + y[:, width:]


def kernel(
    cfg, src, basis, transfer, coupling, blocks, near_pat, far_pat, out,
    buf, bas, nb, buf_a, pair2, buf4, buf5, buf6, wdown, wpath,
    load_sem, nb_sem, halo_send, near_recv, y_recv, z_recv, a_send, a_recv, p_send, p_recv,
    b_send, b_recv, q_send, q_recv, known,
):
    sub, devices, leaf_dev, near = cfg
    rank = basis.shape[1]
    rhs = src.shape[0]
    points = basis.shape[2]
    block = 2 * sub
    block_count = devices // block
    me = lax.axis_index("leaf") * sub + lax.axis_index("sub")
    mine = lax.rem(me, block)
    own_block = me // block
    place_sub = lax.rem(me, sub)
    upper = mine // sub

    def target(dev):
        return (dev // sub, lax.rem(dev, sub))

    def remote(source, dest, send, recv, dev):
        return pltpu.make_async_remote_copy(
            src_ref=source, dst_ref=dest, send_sem=send, recv_sem=recv,
            device_id=target(dev), device_id_type=MESH,
        )

    barrier = pltpu.get_barrier_semaphore()
    peers = []
    for k in range(1, block):
        peers.append(own_block * block + lax.rem(mine + k, block))

    def greet(semaphore, condition, peer):
        @pl.when(condition)
        def _():
            pl.semaphore_signal(semaphore, inc=1, device_id=target(peer), device_id_type=MESH)

    greet(barrier, own_block > 0, me - block)
    greet(barrier, own_block < block_count - 1, me + block)
    for peer in peers:
        pl.semaphore_signal(barrier, inc=1, device_id=target(peer), device_id_type=MESH)

    rounds = block_count - 2

    def make_known(r):
        greet(known.at[r - 1, 0], (own_block > 0) & (own_block + r < block_count), me - block)
        greet(known.at[r - 1, 1], (own_block < block_count - 1) & (own_block >= r), me + block)

    def get_known(r):
        @pl.when(own_block + r + 1 < block_count)
        def _():
            pl.semaphore_wait(known.at[r - 1, 0], 1)

        @pl.when(own_block >= r + 1)
        def _():
            pl.semaphore_wait(known.at[r - 1, 1], 1)

    loads = [
        pltpu.make_async_copy(
            src.at[:, pl.ds(points * leaf, points)], buf.at[2, leaf], load_sem.at[leaf]
        )
        for leaf in range(leaf_dev)
    ]
    base_load = pltpu.make_async_copy(basis, bas, load_sem.at[leaf_dev])
    base_load.start()
    for copy in loads:
        copy.start()
    near_loads = [
        pltpu.make_async_copy(blocks.at[leaf], nb.at[leaf], nb_sem.at[leaf])
        for leaf in range(leaf_dev)
    ]
    for copy in near_loads:
        copy.start()

    def doubled(parts):
        rows = []
        for part in parts:
            row = split(part)
            rows += [row, row]
        return jnp.concatenate(rows, axis=0)

    sides = [transfer[side] for side in range(2)]
    step_weight = jnp.concatenate([doubled([side]) for side in sides], axis=1)
    w_up = {2: doubled(sides)}
    paths = sides
    while len(paths) < max(leaf_dev, block):
        wide = nn(split(jnp.concatenate(paths, axis=0)), step_weight)
        longer = jnp.concatenate(
            [fold(wide[:, : 2 * rank], rank), fold(wide[:, 2 * rank :], rank)], axis=0
        )
        paths = [longer[p * rank : (p + 1) * rank] for p in range(2 * len(paths))]
        w_up[len(paths)] = doubled(paths)

    def lift(parts, span):
        rows = [
            jnp.concatenate(parts[p * span : (p + 1) * span], axis=1)
            for p in range(len(parts) // span)
        ]
        rows = rows[0] if len(rows) == 1 else jnp.concatenate(rows, axis=0)
        lifted = split(fold(nn(rows, w_up[span]), rank))
        return [lifted[p * rhs : (p + 1) * rhs] for p in range(len(parts) // span)]

    base_load.wait()
    for copy in loads:
        copy.wait()
    moment0 = [split(nt(buf[2, leaf], bas[leaf])) for leaf in range(leaf_dev)]
    buf_a[mine] = lift(moment0, leaf_dev)[0]
    two = lift(moment0, leaf_dev // 2)
    pair2[0, 0] = two[0]
    pair2[0, 1] = two[1]

    ends = jnp.where(own_block > 0, 1, 0) + jnp.where(own_block < block_count - 1, 1, 0)
    pl.semaphore_wait(barrier, len(peers) + ends)
    a_copies = []
    for k in range(block - 1, 0, -1):
        a_copies.append(
            remote(
                buf_a.at[mine], buf_a.at[mine], a_send.at[k], a_recv.at[k],
                own_block * block + lax.rem(mine + k, block),
            )
        )
    for copy in a_copies:
        copy.start()
    pair_copy = remote(
        pair2.at[0], pair2.at[1], p_send.at[0], p_recv.at[0], me + 1 - 2 * lax.rem(me, 2)
    )
    pair_copy.start()

    if rounds > 0:
        make_known(1)

    y_slot = 4 - 4 * upper
    z_slot = 4 * upper
    across = me + sub - 2 * sub * upper

    def send_across():
        for leaf in range(leaf_dev):
            remote(
                src.at[:, pl.ds(points * leaf, points)], buf.at[z_slot, leaf],
                halo_send.at[0], y_recv.at[leaf], across,
            ).start()

    outer = (place_sub == 0) | (place_sub == sub - 1)
    pl.when(outer)(send_across)
    for number, step in enumerate((1, -1)):
        @pl.when(place_sub < sub - 1 if step > 0 else place_sub > 0)
        def _(number=number, step=step):
            for leaf in range(leaf_dev):
                remote(
                    src.at[:, pl.ds(points * leaf, points)], buf.at[2 - step, leaf],
                    halo_send.at[1 + number], near_recv.at[number], me + step,
                ).start()

    z_step = block - 2 * block * upper
    z_target = me + z_step
    z_send = (z_target >= 0) & (z_target < devices)
    z_have = (me - z_step >= 0) & (me - z_step < devices)
    first_turn = ((upper == 0) & (place_sub == 0)) | ((upper == 1) & (place_sub == sub - 1))
    second_turn = z_have & (
        ((upper == 0) & (place_sub == sub - 1)) | ((upper == 1) & (place_sub == 0))
    )

    def turn(slot, leaf):
        @pl.when(place_sub == 0)
        def _():
            remote(
                buf.at[slot, leaf], buf.at[3, leaf],
                halo_send.at[4], near_recv.at[1], me + sub - 1,
            ).start()

        @pl.when(place_sub == sub - 1)
        def _():
            remote(
                buf.at[slot, leaf], buf.at[1, leaf],
                halo_send.at[4], near_recv.at[0], me - sub + 1,
            ).start()

    def relay_first(leaf):
        remote(
            buf.at[y_slot, leaf], buf.at[y_slot, leaf], halo_send.at[0], y_recv.at[leaf], across
        ).wait_recv()

        @pl.when(z_send)
        def _():
            remote(
                buf.at[y_slot, leaf], buf.at[z_slot, leaf],
                halo_send.at[3], z_recv.at[leaf], z_target,
            ).start()

        @pl.when(first_turn)
        def _():
            turn(y_slot, leaf)

    def z_wait(leaf):
        remote(
            buf.at[z_slot, leaf], buf.at[z_slot, leaf], halo_send.at[3], z_recv.at[leaf], across
        ).wait_recv()

    def relay_second(leaf):
        @pl.when(second_turn)
        def _():
            z_wait(leaf)
            turn(z_slot, leaf)

    row_starts = [0]
    size = leaf_dev * devices
    while size > 4:
        row_starts.append(row_starts[-1] + size)
        size //= 2

    def weight(offset, row):
        return jnp.full((rhs, 2 * rank), far_pat[offset, row].astype(F32), F32).astype(BF)

    c_hi, c_lo = [], []
    for offset in range(3):
        hi, lo = halves(coupling[offset])
        c_hi += [hi, hi]
        c_lo += [lo, lo]
    w_couple = jnp.concatenate(
        [jnp.concatenate(c_hi, axis=1), jnp.concatenate(c_lo, axis=1)], axis=0
    )

    def couple(groups, rows):
        stacked = [
            jnp.concatenate(
                [weight(offset, row) * members[offset] for offset in range(3)], axis=1
            )
            for members, row in zip(groups, rows)
        ]
        stacked = stacked[0] if len(stacked) == 1 else jnp.concatenate(stacked, axis=0)
        return fold(nt(stacked, w_couple), rank)

    for side in range(2):
        hi, lo = halves(sides[side])
        wdown[side] = jnp.concatenate(
            [jnp.concatenate([hi, hi], axis=1), jnp.concatenate([lo, lo], axis=1)], axis=0
        )
    w_down = jnp.concatenate([wdown[0], wdown[1]], axis=0)

    def descend(field, step):
        return fold(nt(split(field), wdown[lax.rem(me >> step, 2)]), rank)

    def fan_out(field, rows):
        both = nt(split(field), w_down)
        children = []
        for p in range(field.shape[0] // rows):
            row = both[p * rows : (p + 1) * rows]
            children.append(fold(row[:, : 2 * rank], rank))
            children.append(fold(row[:, 2 * rank :], rank))
        return jnp.concatenate(children, axis=0)

    low_levels = leaf_dev.bit_length() - 1
    top_count = len(row_starts) - low_levels - 2
    eye = (
        lax.broadcasted_iota(jnp.int32, (rank, rank), 0)
        == lax.broadcasted_iota(jnp.int32, (rank, rank), 1)
    ).astype(F32)
    chain = eye
    for step in range(top_count, -1, -1):
        if step <= 1:
            chain = descend(chain, step)
        elif step < top_count + 1:
            chain = jnp.concatenate([descend(chain, step), eye], axis=0)
    for _ in range(low_levels):
        chain = fan_out(chain, top_count * rank)
    for leaf in range(leaf_dev):
        for number in range(top_count):
            begin = (leaf * top_count + number) * rank
            piece = split(chain[begin : begin + rank])
            for half in range(2):
                wpath[
                    (2 * number + half) * rank : (2 * number + half + 1) * rank,
                    2 * rank * leaf : 2 * rank * (leaf + 1),
                ] = piece

    def relays(early, late):
        @pl.when(outer)
        def _():
            for step, leaf in early:
                step(leaf)

        if late:
            @pl.when(jnp.logical_not(outer))
            def _():
                for leaf in late:
                    relay_first(leaf)

    queue = [(relay_first, leaf) for leaf in range(leaf_dev)]
    queue += [(relay_second, leaf) for leaf in range(leaf_dev)]
    half = leaf_dev // 2
    relays(queue[:half], [])

    locals_low = []
    level_vals, level_id = moment0, 0
    while (leaf_dev >> level_id) >= 4:
        if level_id:
            level_vals = lift(level_vals, 2)
        count = leaf_dev >> level_id
        locals_low.append(
            couple(
                [
                    [level_vals[c // 4 * 4 + (c + offset) % 4] for offset in range(1, 4)]
                    for c in range(count)
                ],
                [row_starts[level_id] + me * count + c for c in range(count)],
            )
        )
        level_id += 1

    for r in range(1, rounds + 1):
        get_known(r)
        if r < rounds:
            make_known(r + 1)

    for k in range(block - 1, 0, -1):
        source = lax.rem(mine - k + block, block)
        remote(
            buf_a.at[source], buf_a.at[source], a_send.at[k], a_recv.at[k], me ^ 1
        ).wait_recv()
    eight = [buf_a[p] for p in range(block)]
    buf6[own_block] = lift(eight, block)[0]
    b_copies = []
    for k in range(block_count - 1, 0, -1):
        b_copies.append(
            remote(
                buf6.at[own_block], buf6.at[own_block], b_send.at[k], b_recv.at[k],
                lax.rem(own_block + k, block_count) * block + mine,
            )
        )
    for copy in b_copies:
        copy.start()
    five = lift(eight, block // 2)
    for p in range(2):
        buf5[p] = five[p]
    q_copy = remote(
        buf5.at[pl.ds(0, 2)], buf5.at[pl.ds(2, 2)], q_send.at[0], q_recv.at[0],
        (own_block + 1 - 2 * lax.rem(own_block, 2)) * block + mine,
    )
    q_copy.start()
    pl.when(jnp.logical_not(outer))(send_across)
    relays(queue[half:leaf_dev], [])
    for p, part in enumerate(lift(eight, 2)):
        buf4[p] = part

    pair_copy.wait()
    members2 = two + [pair2[1, 0], pair2[1, 1]]
    groups = [[members2[(c + offset) % 4] for offset in range(1, 4)] for c in range(2)]
    rows = [row_starts[level_id] + me * 2 + c for c in range(2)]
    level_id += 1
    groups.append(
        [buf_a[upper * sub + lax.rem(place_sub + offset, 4)] for offset in range(1, 4)]
    )
    rows.append(row_starts[level_id] + me)
    groups.append([buf4[lax.rem(mine // 2 + offset, 4)] for offset in range(1, 4)])
    rows.append(row_starts[level_id + 1] + me // 2)
    relays(queue[leaf_dev : leaf_dev + 2], range(0, 2))
    middle = couple(groups, rows)
    locals_low.append(middle[: 2 * rhs])
    field = middle[2 * rhs : 3 * rhs] + descend(middle[3 * rhs :], 0)
    for step in range(len(locals_low) - 1, -1, -1):
        field = locals_low[step] + fan_out(field, rhs)
    relays(queue[leaf_dev + 2 : leaf_dev + half], range(2, half))

    for copy in near_loads:
        copy.wait()
    first = [nt(buf[2, leaf], nb[leaf, 0]) for leaf in range(leaf_dev)]
    relays(queue[leaf_dev + half :], range(half, leaf_dev))

    for k in range(block_count - 1, 0, -1):
        source = lax.rem(own_block - k + block_count, block_count)
        remote(
            buf6.at[source], buf6.at[source], b_send.at[k], b_recv.at[k], me ^ 1
        ).wait_recv()
    q_copy.wait()
    groups = [[buf5[lax.rem(upper + offset, 4)] for offset in range(1, 4)]]
    rows = [row_starts[level_id + 2] + me // sub]
    first_six = level_id + 3
    start, span, level = 0, block_count, first_six
    while True:
        own = own_block >> (level - first_six)
        groups.append(
            [
                buf6[start + own // 4 * 4 + lax.rem(lax.rem(own, 4) + offset, 4)]
                for offset in range(1, 4)
            ]
        )
        rows.append(row_starts[level] + own)
        if span <= 4:
            break
        for p, part in enumerate(lift([buf6[start + p] for p in range(span)], 2)):
            buf6[start + span + p] = part
        start, span, level = start + span, span // 2, level + 1
    groups, rows = groups[::-1], rows[::-1]
    top = split(couple(groups, rows))
    top = jnp.concatenate([top[p * rhs : (p + 1) * rhs] for p in range(top_count)], axis=1)
    spread = nn(top, wpath[...])
    partial = []
    for leaf in range(leaf_dev):
        whole = split(
            field[leaf * rhs : (leaf + 1) * rhs]
            + fold(spread[:, 2 * rank * leaf : 2 * rank * (leaf + 1)], rank)
        )
        twice = jnp.concatenate([bas[leaf], bas[leaf]], axis=0)
        partial.append(first[leaf] + nn(whole, twice))

    @pl.when(z_have & jnp.logical_not(second_turn))
    def _():
        for leaf in range(leaf_dev):
            z_wait(leaf)

    for number, step in enumerate((-1, 1)):
        @pl.when(me > 0 if step < 0 else me < devices - 1)
        def _(number=number, step=step):
            pltpu.make_async_copy(buf.at[2 + step], buf.at[2 + step], near_recv.at[number]).wait()
    for leaf in range(leaf_dev):
        acc = partial[leaf]
        for s in range(1, near):
            index = near_pat[s, leaf]
            gap = index // leaf_dev - me
            place = jnp.where(
                gap == -sub, 0, jnp.where(gap == -1, 1, jnp.where(gap == 0, 2, jnp.where(gap == 1, 3, 4)))
            )
            acc = acc + nt(buf[place, lax.rem(index, leaf_dev)], nb[leaf, s])
        out[:, points * leaf : points * (leaf + 1)] = acc.astype(out.dtype)

    sent = (
        me >= 0, place_sub < sub - 1, place_sub > 0, z_send, first_turn | second_turn,
    )
    for number, condition in enumerate(sent):
        @pl.when(condition)
        def _(number=number):
            pltpu.make_async_copy(buf.at[2], buf.at[2], halo_send.at[number]).wait()
    for copy in a_copies + b_copies:
        copy.wait_send()


def shards(sizes, sources, leaf_basis, transfer, coupling, near_blocks, near_pattern, far_pattern):
    sub, devices = sizes
    leaf_dev, points, rank = leaf_basis.shape
    rhs = sources.shape[1]
    near = near_blocks.shape[1]
    block = 2 * sub
    block_count = devices // block
    top_count = block_count.bit_length() - 1
    vmem = pl.BlockSpec(memory_space=pltpu.VMEM)
    smem = pl.BlockSpec(memory_space=pltpu.SMEM)
    hbm = pl.BlockSpec(memory_space=pl.ANY)
    dma = pltpu.SemaphoreType.DMA
    result = pl.pallas_call(
        functools.partial(kernel, (sub, devices, leaf_dev, near)),
        out_shape=pltpu.VMEM((rhs, leaf_dev * points), BF),
        in_specs=[hbm, hbm, vmem, vmem, hbm, smem, smem],
        out_specs=vmem,
        scratch_shapes=[
            pltpu.VMEM((5, leaf_dev, rhs, points), BF),
            pltpu.VMEM((leaf_dev, rank, points), BF),
            pltpu.VMEM((leaf_dev, near, points, points), BF),
            pltpu.VMEM((block, rhs, 2 * rank), BF),
            pltpu.VMEM((2, 2, rhs, 2 * rank), BF),
            pltpu.VMEM((4, rhs, 2 * rank), BF),
            pltpu.VMEM((4, rhs, 2 * rank), BF),
            pltpu.VMEM((2 * block_count, rhs, 2 * rank), BF),
            pltpu.VMEM((2, 2 * rank, 2 * rank), BF),
            pltpu.VMEM((2 * top_count * rank, 2 * rank * leaf_dev), BF),
            dma((leaf_dev + 1,)),
            dma((leaf_dev,)),
            dma((5,)),
            dma((2,)),
            dma((leaf_dev,)),
            dma((leaf_dev,)),
            dma((block,)),
            dma((block,)),
            dma((1,)),
            dma((1,)),
            dma((block_count,)),
            dma((block_count,)),
            dma((1,)),
            dma((1,)),
            pltpu.SemaphoreType.REGULAR((max(block_count - 2, 1), 2)),
        ],
        compiler_params=pltpu.CompilerParams(collective_id=0, has_side_effects=True),
    )(
        sources.T,
        leaf_basis.transpose(0, 2, 1),
        transfer,
        coupling,
        near_blocks,
        near_pattern.T,
        far_pattern.T,
    )
    return result.T


def solution(mesh):
    placed = (
        P(("leaf", "sub"), None),
        P(("leaf", "sub"), None, None),
        P(),
        P(),
        P(("leaf", "sub"), None, None, None),
        P(("leaf", "sub"), None),
        P(),
    )
    sizes = (mesh.shape["sub"], mesh.shape["leaf"] * mesh.shape["sub"])
    return jax.shard_map(
        functools.partial(shards, sizes),
        mesh=mesh, in_specs=placed, out_specs=P(("leaf", "sub"), None), check_vma=False,
    )
```
